32 devices in a mesh: dp: 2 (over y), section: 4 (over z), mp: 4 (over x, core).
Axes of the slice: x: 2, y: 2, z: 4, core: 2. Of those that a mesh axis runs over, the one named last changes fastest.
Arguments:
- token_ids: int32 [32, 32], P('dp'), may hold values from 0 to 65535
- members: int32 [32], replicated, may hold values from 0 to 31, each once
- owners: int32 [4], replicated, may hold values from 0 to 3, each once
- embed_table: bfloat16 [4096, 65536], P('mp', 'section'), may hold values from -6 to 6
- norm_gain: float32 [4, 4096], P('section'), may hold values from 0.5 to 2
- gate_weight: bfloat16 [4, 4096, 10240], P('section', None, 'mp'), may hold values from -0.09375 to 0.09375
- up_weight: bfloat16 [4, 4096, 10240], P('section', None, 'mp'), may hold values from -0.09375 to 0.09375
- down_weight: bfloat16 [4, 4096, 10240], P('section', None, 'mp'), may hold values from -0.078125 to 0.078125
- final_gain: float32 [4096], replicated, may hold values from 0.5 to 2
- head_weight: bfloat16 [4096, 4096], P(None, 'mp'), may hold values from -0.0014648438 to 0.0014648438
Outputs:
- wins: float32 [4, 8, 8], P('dp', 'section')
The draws below stay inside these ranges and needn't reach their ends.
Inputs may be any that keep to these rules, and one draw needn't show every extreme that they name: Prompt p's responses are members[8 * p] to members[8 * p + 7]; each response belongs to one prompt. `owners`: each slot holds one prompt.
All inputs are finite; a program needn't handle non-finite values.
Results may differ from the reference program's by a relative error of at most 0.028.
Values may be sent and summed in bfloat16 or wider, within the bound.
A program may use at most 192 MiB of HBM per device.

```python
import math
import jax
import jax.numpy as jnp
from jax import lax

D = 4096
FF = 10240
VOCAB = 65536
LENGTH = 32
GROUP = 8
LAYERS = 4
RESPONSES = 32
PROMPTS = 4
N_MP = 4


def place_ends(drawn, own_key, smallest, largest):
    longest = drawn.shape.index(max(drawn.shape))
    spots = []
    for shift in (0, 1):
        where = [jax.random.randint(jax.random.fold_in(own_key, axis), (), 0, length) for axis, length in enumerate(drawn.shape)]
        where[longest] = (where[longest] + shift) % drawn.shape[longest]
        spots.append(tuple(where))
    return drawn.at[spots[0]].set(smallest).at[spots[1]].set(largest)


def raised(drawn, key, source, target, blocks, factor):
    def block_of(position):
        return (jnp.arange(drawn.shape[position]) // (drawn.shape[position] // blocks)).reshape((-1,) + (1,) * (drawn.ndim - 1 - position))

    first = jax.random.permutation(key, blocks)[block_of(target)]
    second = (block_of(target) + blocks // 2) % blocks
    return jnp.where((block_of(source) == first) | (block_of(source) == second), factor * drawn, drawn)


def level_of(own_key, extent, split, smallest, top_value):
    def one(dim, shards_of):
        steps = jax.random.uniform(jax.random.fold_in(jax.random.fold_in(own_key, 6), dim), (shards_of,), jnp.float32, smallest / len(split), top_value / len(split))
        return jnp.repeat(jnp.exp(steps), extent[dim] // shards_of).reshape((-1,) + (1,) * (len(extent) - dim - 1))

    loudness = one(*split[0])
    for cut in split[1:]:
        loudness = loudness * one(*cut)
    return loudness


def noise(key, extent, scale, limit, split=(), dtype=jnp.bfloat16):
    level = level_of(key, extent, split, -0.22, 0.18) if split else 1.0
    result = jax.random.normal(key, extent, jnp.float32) * scale * level
    return jnp.minimum(jnp.maximum(result, -limit), limit).astype(dtype)


def heavy_noise(rng, dims, scale, bound, split, heavy, dtype=jnp.bfloat16):
    drawn = scale * jax.random.normal(rng, dims, jnp.float32)
    if split:
        drawn = drawn * level_of(rng, dims, split, -0.22, 0.18)
    return jnp.clip(raised(drawn, jax.random.fold_in(rng, 3), *heavy), -bound, bound).astype(dtype)


def setup_inputs(seed: int = 0) -> dict:
    key_list = jax.random.split(jax.random.key(seed), 11)
    token_ids = place_ends(jax.random.randint(key_list[0], (RESPONSES, LENGTH), 0, VOCAB), jax.random.fold_in(key_list[0], 1), 0, VOCAB - 1).astype(jnp.int32)
    members = jax.random.permutation(key_list[1], RESPONSES).astype(jnp.int32)
    owners = jax.random.permutation(key_list[2], PROMPTS).astype(jnp.int32)
    embed_table = noise(key_list[3], (D, VOCAB), 1.0, 6.0, ((0, 4), (1, 4)))
    norm_gain = jnp.clip(jnp.exp(math.log(2.0) - 1.3862944 * jax.random.uniform(key_list[4], (LAYERS, D), jnp.float32) ** level_of(key_list[4], (LAYERS, D), ((0, 4),), -0.2, 0.2)), 0.5, 2.0)
    gate_weight = noise(key_list[5], (LAYERS, D, FF), D ** -0.5, 0.09375, ((0, 4), (2, 4)))
    up_weight = noise(key_list[6], (LAYERS, D, FF), D ** -0.5, 0.09375, ((0, 4), (2, 4)))
    down_weight = heavy_noise(key_list[7], (LAYERS, D, FF), FF ** -0.5, 0.078125, ((0, 4), (2, 4)), (2, 1, 4, 2.0))
    final_gain = jnp.clip(jnp.exp(jax.random.uniform(key_list[8], (D,), jnp.float32, math.log(0.5), math.log(2.0))), 0.5, 2.0)
    head_weight = noise(key_list[9], (D, D), (D * D) ** -0.5, 0.0014648438, ((1, 4),))
    return dict(token_ids=token_ids, members=members, owners=owners, embed_table=embed_table, norm_gain=norm_gain, gate_weight=gate_weight, up_weight=up_weight, down_weight=down_weight, final_gain=final_gain, head_weight=head_weight)


norm_eps = 1e-05
final_eps = 1e-06

def contract_rows(weights, acts):
    return lax.dot_general(weights, acts, (((0,), (0,)), ((), ())), preferred_element_type=jnp.float32)

def reference(token_ids, members, owners, embed_table, norm_gain, gate_weight, up_weight, down_weight, final_gain, head_weight):
    state = jnp.take(embed_table, token_ids.reshape(-1), axis=1)
    block = FF // N_MP
    for layer in range(LAYERS):
        wide = state.astype(jnp.float32)
        scaled = (wide * norm_gain[layer][:, None]).astype(jnp.bfloat16)
        inverse = lax.rsqrt(lax.optimization_barrier(jnp.mean(wide * wide, axis=0, keepdims=True)) + norm_eps)
        gate = contract_rows(gate_weight[layer], scaled) * inverse
        upper = contract_rows(up_weight[layer], scaled) * inverse
        hidden = (jax.nn.silu(gate) * upper).astype(jnp.bfloat16)
        w_down = down_weight[layer]

        def add_block(index, total):
            start = (index * block).astype(jnp.int32)
            part = jnp.dot(lax.dynamic_slice_in_dim(w_down, start, block, 1), lax.dynamic_slice_in_dim(hidden, start, block, 0), preferred_element_type=jnp.float32)
            rounded = lax.optimization_barrier(part.astype(jnp.bfloat16))
            return total + rounded.astype(jnp.float32)
        total = lax.fori_loop(jnp.int32(0), jnp.int32(N_MP), add_block, jnp.zeros(wide.shape, jnp.float32))
        state = (wide + total).astype(jnp.bfloat16)
    pooled = lax.optimization_barrier(jnp.mean(state.astype(jnp.float32).reshape(D, RESPONSES, LENGTH), axis=2))
    factor = lax.rsqrt(lax.optimization_barrier(jnp.mean(pooled * pooled, axis=0, keepdims=True)) + final_eps)
    normed = (pooled * factor * final_gain[:, None]).astype(jnp.bfloat16)
    projected = contract_rows(head_weight, normed)
    scores = lax.dot_general(projected, normed.astype(jnp.float32), (((0,), (0,)), ((), ())), precision=lax.Precision.HIGHEST, preferred_element_type=jnp.float32)
    preference = jax.nn.sigmoid(scores - scores.T)
    groups = members.reshape(PROMPTS, GROUP)
    tiles = preference[groups[:, :, None], groups[:, None, :]]
    return jnp.zeros((PROMPTS, GROUP, GROUP), jnp.float32).at[owners].set(tiles)
```

```python
import functools

import jax
import jax.numpy as jnp
from jax import lax
from jax.experimental import pallas as pl
from jax.experimental.pallas import tpu as pltpu
from jax.sharding import PartitionSpec as P

GROUP = 8
BATCHES = 2
CHUNK = 256

norm_eps = 1e-05
final_eps = 1e-06
MESH = pl.DeviceIdType.MESH


def broadcast(block, axis, source):
    block = jnp.where(lax.axis_index(axis) == source, block, jnp.zeros_like(block))
    return lax.psum(block, axis)


def contract_rows(weights, acts):
    return lax.dot_general(
        weights, acts, (((0,), (0,)), ((), ())), preferred_element_type=jnp.float32
    )


def pipe_kernel(
    sections,
    parts,
    x0,
    gain,
    wg,
    wu,
    wd,
    out,
    xall,
    wgb,
    wub,
    wdb,
    accg,
    accu,
    hid,
    xs,
    sq,
    sibs,
    sibr,
    crs,
    crr,
    pown,
    gsem,
    usem,
    dsem,
    x0sem,
    zsend,
    zrecv,
    agsend,
    agrecv,
    fwdsend,
    sibsend,
    sibrecv,
    crsend,
    crrecv,
):
    batches, steps, tokens, chunk = x0.shape
    chips = parts // 2
    width = parts * steps * chunk
    n_fb, _, fb_size = accg.shape
    sec = lax.axis_index("section")
    me = lax.axis_index("mp")
    core = lax.rem(me, 2)
    chip = lax.div(me, 2)
    sib = me + 1 - 2 * core

    def peer(d):
        return lax.rem(chip + d, chips) * 2 + core

    def remote(src, dst, send, recv, target):
        return pltpu.make_async_remote_copy(
            src_ref=src,
            dst_ref=dst,
            send_sem=send,
            recv_sem=recv,
            device_id=target,
            device_id_type=MESH,
        )

    def gcopy(i):
        return pltpu.make_async_copy(wg.at[:, i % steps], wgb.at[i % 2], gsem.at[i % 2])

    def ucopy(i):
        return pltpu.make_async_copy(wu.at[:, i % steps], wub.at[i % 2], usem.at[i % 2])

    def dcopy(q):
        return pltpu.make_async_copy(wd.at[:, q], wdb.at[q], dsem.at[q])

    def x0copy(m, q):
        return pltpu.make_async_copy(x0.at[m, q], xall.at[m, q, me], x0sem.at[m, q])

    def zcopy(m, q):
        return remote(
            out.at[m, q], xall.at[m, q, me], zsend.at[m, q], zrecv.at[m, q], {"section": sec + 1}
        )

    def agcopy(m, q, d):
        slot = xall.at[m, q, me]
        target = sib if d == 0 else peer(d)
        return remote(slot, slot, agsend.at[m, q, d], agrecv.at[m, q, me], {"mp": target})

    def fwdcopy(m, q, d):
        slot = xall.at[m, q, peer(d)]
        return remote(slot, slot, fwdsend.at[m, q, d], agrecv.at[m, q, peer(d)], {"mp": sib})

    def agwait(m, q, owner):
        slot = xall.at[m, q, owner]
        remote(slot, slot, agsend.at[m, q, 0], agrecv.at[m, q, owner], {"mp": sib}).wait_recv()

    def sibcopy(m, q, c):
        return remote(
            sibs.at[m, q, c], sibr.at[m, q, c], sibsend.at[m, q, c], sibrecv.at[m, q, c], {"mp": sib}
        )

    def crcopy(m, q, d):
        return remote(
            crs.at[m, q, d - 1],
            crr.at[m, q, d - 1],
            crsend.at[m, q, d - 1],
            crrecv.at[m, q, d - 1],
            {"mp": peer(d)},
        )

    total_steps = batches * steps
    for i in range(min(2, total_steps)):
        gcopy(i).start()
        ucopy(i).start()
    for q in range(steps):
        dcopy(q).start()

    @pl.when(sec == 0)
    def _():
        for m in range(batches):
            for q in range(steps):
                x0copy(m, q).start()

    barrier = pltpu.get_barrier_semaphore()
    pl.semaphore_signal(barrier, inc=1, device_id={"mp": sib}, device_id_type=MESH)
    for d in range(1, chips):
        pl.semaphore_signal(barrier, inc=1, device_id={"mp": peer(d)}, device_id_type=MESH)

    for turn in (1, sections - 1):
        around = lax.rem(sec + turn, sections)
        pl.semaphore_signal(barrier, inc=1, device_id={"section": around}, device_id_type=MESH)
    pl.semaphore_wait(barrier, chips + 2)

    def own_arrive(m, q):
        @pl.when(sec == 0)
        def _():
            x0copy(m, q).wait()

        @pl.when(sec > 0)
        def _():
            zcopy(m, q).wait_recv()

        for d in range(1, chips):
            agcopy(m, q, d).start()
        agcopy(m, q, 0).start()

    def gate_step(m, q):
        i = m * steps + q
        if q + 1 < steps:
            own_arrive(m, q + 1)
        for d in range(1, chips):
            agwait(m, q, peer(d))
            fwdcopy(m, q, d).start()
        for c in range(chips):
            agwait(m, q, 2 * c + 1 - core)
        squares = jnp.zeros(sq.shape, jnp.float32) if q == 0 else sq[...]
        lanes = sq.shape[1]
        for o in range(parts):
            x = xall[m, q, o].astype(jnp.float32)
            for lane in range(0, chunk, lanes):
                piece = x[:, lane : lane + lanes]
                squares = squares + piece * piece
            xs[:, o * chunk : (o + 1) * chunk] = (x * gain[o, q]).astype(jnp.bfloat16)
        sq[...] = squares
        gcopy(i).wait()
        ucopy(i).wait()

        def block(fb, carry):
            cols = pl.ds(pl.multiple_of(fb * fb_size, fb_size), fb_size)
            for acc, buf in ((accg, wgb), (accu, wub)):
                w = buf[i % 2, :, :, cols].reshape(parts * chunk, fb_size)
                term = jnp.dot(xs[...], w, preferred_element_type=jnp.float32)
                acc[fb] = term if q == 0 else acc[fb] + term
            return carry

        lax.fori_loop(0, n_fb, block, 0)
        if i + 2 < total_steps:
            gcopy(i + 2).start()
            ucopy(i + 2).start()

    def act_step():
        mean = jnp.sum(sq[...], axis=1, keepdims=True) / width
        inverse = lax.rsqrt(mean + norm_eps)

        def block(fb, carry):
            cols = pl.ds(pl.multiple_of(fb * fb_size, fb_size), fb_size)
            g = accg[fb] * inverse
            u = accu[fb] * inverse
            hid[:, cols] = (g / (1.0 + jnp.exp(-g)) * u).astype(jnp.bfloat16)
            return carry

        lax.fori_loop(0, n_fb, block, 0)

    def down(q, owner):
        return lax.dot_general(
            hid[...], wdb[q, owner], (((1,), (1,)), ((), ())), preferred_element_type=jnp.float32
        )

    def finish(m, q):
        sibcopy(m, q, chip).wait_recv()
        new = pown[q % 2, 0] + sibr[m, q, chip].astype(jnp.float32)
        for d in range(1, chips):
            crcopy(m, q, d).wait_recv()
            new = new + crr[m, q, d - 1].astype(jnp.float32)
        new = xall[m, q, me].astype(jnp.float32) + new
        out[m, q] = new.astype(jnp.bfloat16)

        @pl.when(sec < sections - 1)
        def _():
            zcopy(m, q).start()

    def down_step(m, q):
        if m == 0:
            dcopy(q).wait()

        def to_sibling(c, carry):
            sibs[m, q, c] = down(q, 2 * c + 1 - core).astype(jnp.bfloat16)
            sibcopy(m, q, c).start()
            return carry

        lax.fori_loop(0, chips, to_sibling, 0)

        def to_own(d, carry):
            pown[q % 2, d] = down(q, peer(d))
            return carry

        lax.fori_loop(0, chips, to_own, 0)
        for d in range(1, chips):
            c = lax.rem(chip + d, chips)
            sibcopy(m, q, c).wait_recv()
            both = pown[q % 2, d] + sibr[m, q, c].astype(jnp.float32)
            crs[m, q, d - 1] = both.astype(jnp.bfloat16)
            crcopy(m, q, d).start()
        if q > 0:
            finish(m, q - 1)

    for m in range(batches):
        own_arrive(m, 0)
        for q in range(steps):
            gate_step(m, q)
        act_step()
        for q in range(steps):
            down_step(m, q)
        finish(m, steps - 1)

    for m in range(batches):
        for q in range(steps):
            for c in range(chips):
                agcopy(m, q, c).wait_send()
                sibcopy(m, q, c).wait_send()
            for d in range(1, chips):
                fwdcopy(m, q, d).wait_send()
                crcopy(m, q, d).wait_send()

    @pl.when(sec < sections - 1)
    def _():
        for m in range(batches):
            for q in range(steps):
                zcopy(m, q).wait_send()


def pipeline(embedded, gain, w_gate, w_up, w_down):
    sections = lax.axis_size("section")
    parts = lax.axis_size("mp")
    chips = parts // 2
    all_tokens, local = embedded.shape
    hidden = w_gate.shape[1]
    width = gain.shape[0]
    batches = BATCHES
    tokens = all_tokens // batches
    chunk = min(CHUNK, local)
    steps = local // chunk
    fb_size = next(size for size in (512, 256, 128, hidden) if hidden % size == 0)
    x0 = embedded.reshape(batches, tokens, steps, chunk).transpose(0, 2, 1, 3)
    split = (parts, steps, chunk, hidden)
    bf16, f32 = jnp.bfloat16, jnp.float32
    vmem = pl.BlockSpec(memory_space=pltpu.VMEM)
    hbm = pl.BlockSpec(memory_space=pltpu.MemorySpace.HBM)
    dma = pltpu.SemaphoreType.DMA
    per_chip = (batches, steps, chips)
    others = max(1, chips - 1)
    tile = (tokens, chunk)
    out = pl.pallas_call(
        functools.partial(pipe_kernel, sections, parts),
        out_shape=jax.ShapeDtypeStruct(x0.shape, bf16),
        in_specs=[vmem, vmem, hbm, hbm, hbm],
        out_specs=vmem,
        scratch_shapes=[
            pltpu.VMEM((batches, steps, parts) + tile, bf16),
            pltpu.VMEM((2, parts, chunk, hidden), bf16),
            pltpu.VMEM((2, parts, chunk, hidden), bf16),
            pltpu.VMEM((steps, parts, chunk, hidden), bf16),
            pltpu.VMEM((hidden // fb_size, tokens, fb_size), f32),
            pltpu.VMEM((hidden // fb_size, tokens, fb_size), f32),
            pltpu.VMEM((tokens, hidden), bf16),
            pltpu.VMEM((tokens, parts * chunk), bf16),
            pltpu.VMEM((tokens, min(128, chunk)), f32),
            pltpu.VMEM(per_chip + tile, bf16),
            pltpu.VMEM(per_chip + tile, bf16),
            pltpu.VMEM((batches, steps, others) + tile, bf16),
            pltpu.VMEM((batches, steps, others) + tile, bf16),
            pltpu.VMEM((2, chips) + tile, f32),
            dma((2,)),
            dma((2,)),
            dma((steps,)),
            dma((batches, steps)),
            dma((batches, steps)),
            dma((batches, steps)),
            dma(per_chip),
            dma((batches, steps, parts)),
            dma(per_chip),
            dma(per_chip),
            dma(per_chip),
            dma(per_chip),
            dma(per_chip),
        ],
        compiler_params=pltpu.CompilerParams(
            collective_id=0, has_side_effects=True, vmem_limit_bytes=67043328
        ),
    )(
        x0,
        gain.reshape(parts, steps, 1, chunk),
        w_gate.reshape(split),
        w_up.reshape(split),
        w_down.reshape(split),
    )
    return out.transpose(1, 3, 0, 2).reshape(local, all_tokens)


def per_device(
    token_ids,
    members,
    owners,
    embed_table,
    norm_gain,
    gate_weight,
    up_weight,
    down_weight,
    final_gain,
    head_weight,
):
    sections = lax.axis_size("section")
    section = lax.axis_index("section")
    vocab_part = embed_table.shape[1]
    flat = token_ids.reshape(-1)
    local_ids = flat - section * vocab_part
    places = jnp.arange(vocab_part, dtype=jnp.int32)
    chosen_ids = (local_ids[:, None] == places[None, :]).astype(jnp.bfloat16)
    picked = lax.dot_general(
        chosen_ids, embed_table, (((1,), (1,)), ((), ())), preferred_element_type=jnp.float32
    )
    embedded = lax.psum(picked.astype(jnp.bfloat16), "section")
    final = pipeline(embedded, norm_gain[0], gate_weight[0], up_weight[0], down_weight[0])
    responses_here = token_ids.shape[0]
    length = token_ids.shape[1]
    pooled = jnp.mean(
        final.astype(jnp.float32).reshape(final.shape[0], responses_here, length), axis=2
    )
    groups_count = lax.axis_size("dp")
    parts = lax.axis_size("mp")
    stacked = lax.all_gather(pooled[None], ("dp", "mp"), axis=0, tiled=True)
    stacked = stacked.reshape(groups_count, parts, pooled.shape[0], responses_here)
    everyone = jnp.transpose(stacked, (1, 2, 0, 3)).reshape(
        parts * pooled.shape[0], groups_count * responses_here
    )
    factor = lax.rsqrt(jnp.mean(everyone * everyone, axis=0, keepdims=True) + final_eps)
    normed = (everyone * factor * final_gain[:, None]).astype(jnp.bfloat16)
    head_cols = head_weight.shape[1]
    projected = contract_rows(head_weight, normed)
    mine = lax.dynamic_slice_in_dim(normed, lax.axis_index("mp") * head_cols, head_cols).astype(
        jnp.float32
    )
    partial_scores = lax.dot_general(
        projected,
        mine,
        (((0,), (0,)), ((), ())),
        precision=lax.Precision.HIGHEST,
        preferred_element_type=jnp.float32,
    )
    scores = lax.psum(partial_scores, "mp")
    scores = broadcast(scores, "section", sections - 1)
    preference = jax.nn.sigmoid(scores - scores.T)
    prompt_count = owners.shape[0]
    local_prompts = prompt_count // lax.axis_size("dp")
    rows_local = GROUP // sections
    slot_here = lax.axis_index("dp") * local_prompts + jnp.arange(local_prompts, dtype=jnp.int32)
    match = (owners[None, :] == slot_here[:, None]).astype(jnp.int32)
    prompt_here = jnp.sum(match * jnp.arange(prompt_count, dtype=jnp.int32)[None, :], axis=1)
    groups = members.reshape(prompt_count, GROUP)
    chosen = groups[prompt_here]
    row_ids = lax.dynamic_slice_in_dim(chosen, section * rows_local, rows_local, 1)
    return preference[row_ids[:, :, None], chosen[:, None, :]]


def solution(mesh):
    placed = (
        P("dp", None),
        P(),
        P(),
        P("mp", "section"),
        P("section", None),
        P("section", None, "mp"),
        P("section", None, "mp"),
        P("section", None, "mp"),
        P(),
        P(None, "mp"),
    )
    return jax.shard_map(
        per_device, mesh=mesh, in_specs=placed, out_specs=P("dp", "section", None), check_vma=False
    )
```

```python
import functools

import jax
import jax.numpy as jnp
from jax import lax
from jax.experimental import pallas as pl
from jax.experimental.pallas import tpu as pltpu
from jax.sharding import PartitionSpec as P

GROUP = 8
BATCHES = 2
CHUNK = 256

norm_eps = 1e-05
final_eps = 1e-06
MESH = pl.DeviceIdType.MESH


def contract_rows(weights, acts):
    return lax.dot_general(
        weights, acts, (((0,), (0,)), ((), ())), preferred_element_type=jnp.float32
    )


def pipe_kernel(
    sections,
    parts,
    x0,
    gain,
    wg,
    wu,
    wd,
    pooled,
    out,
    xall,
    wgb,
    wub,
    wdb,
    accg,
    accu,
    hid,
    xs,
    sq,
    sibs,
    sibr,
    crs,
    crr,
    pown,
    gsem,
    usem,
    dsem,
    ering,
    esend,
    erecv,
    zsend,
    zrecv,
    agsend,
    agrecv,
    fwdsend,
    sibsend,
    sibrecv,
    crsend,
    crrecv,
):
    batches, steps, tokens, chunk = x0.shape
    chips = parts // 2
    width = parts * steps * chunk
    n_fb, _, fb_size = accg.shape
    sec = lax.axis_index("section")
    me = lax.axis_index("mp")
    core = lax.rem(me, 2)
    chip = lax.div(me, 2)
    sib = me + 1 - 2 * core

    def peer(d):
        return lax.rem(chip + d, chips) * 2 + core

    def remote(src, dst, send, recv, target):
        return pltpu.make_async_remote_copy(
            src_ref=src,
            dst_ref=dst,
            send_sem=send,
            recv_sem=recv,
            device_id=target,
            device_id_type=MESH,
        )

    def gcopy(i):
        return pltpu.make_async_copy(wg.at[:, i % steps], wgb.at[i % 2], gsem.at[i % 2])

    def ucopy(i):
        return pltpu.make_async_copy(wu.at[:, i % steps], wub.at[i % 2], usem.at[i % 2])

    def dcopy(q):
        return pltpu.make_async_copy(wd.at[:, q], wdb.at[q], dsem.at[q])

    def ecopy(m, q, src):
        target = {"section": sec - 1}
        return remote(src, ering.at[m, q], esend.at[m, q], erecv.at[m, q], target)

    def zcopy(m, q):
        return remote(
            out.at[m, q], xall.at[m, q, me], zsend.at[m, q], zrecv.at[m, q], {"section": sec + 1}
        )

    def agcopy(m, q, d):
        slot = xall.at[m, q, me]
        target = sib if d == 0 else peer(d)
        return remote(slot, slot, agsend.at[m, q, d], agrecv.at[m, q, me], {"mp": target})

    def fwdcopy(m, q, d):
        slot = xall.at[m, q, peer(d)]
        return remote(slot, slot, fwdsend.at[m, q, d], agrecv.at[m, q, peer(d)], {"mp": sib})

    def agwait(m, q, owner):
        slot = xall.at[m, q, owner]
        remote(slot, slot, agsend.at[m, q, 0], agrecv.at[m, q, owner], {"mp": sib}).wait_recv()

    def sibcopy(m, q, c):
        return remote(
            sibs.at[m, q, c], sibr.at[m, q, c], sibsend.at[m, q, c], sibrecv.at[m, q, c], {"mp": sib}
        )

    def crcopy(m, q, d):
        return remote(
            crs.at[m, q, d - 1],
            crr.at[m, q, d - 1],
            crsend.at[m, q, d - 1],
            crrecv.at[m, q, d - 1],
            {"mp": peer(d)},
        )

    total_steps = batches * steps
    for i in range(min(2, total_steps)):
        gcopy(i).start()
        ucopy(i).start()
    for q in range(steps):
        dcopy(q).start()

    barrier = pltpu.get_barrier_semaphore()
    pl.semaphore_signal(barrier, inc=1, device_id={"mp": sib}, device_id_type=MESH)
    for d in range(1, chips):
        pl.semaphore_signal(barrier, inc=1, device_id={"mp": peer(d)}, device_id_type=MESH)

    for turn in (1, sections - 1):
        around = lax.rem(sec + turn, sections)
        pl.semaphore_signal(barrier, inc=1, device_id={"section": around}, device_id_type=MESH)
    pl.semaphore_wait(barrier, chips + 2)

    def own_arrive(m, q):
        @pl.when(sec == 0)
        def _():
            if sections > 1:
                ecopy(m, q, x0.at[m, q]).wait_recv()
                xall[m, q, me] = ering[m, q] + x0[m, q]
            else:
                xall[m, q, me] = x0[m, q]

        @pl.when(sec > 0)
        def _():
            zcopy(m, q).wait_recv()

        for d in range(1, chips):
            agcopy(m, q, d).start()
        agcopy(m, q, 0).start()

    def gate_step(m, q):
        i = m * steps + q
        if q + 1 < steps:
            own_arrive(m, q + 1)
        for d in range(1, chips):
            agwait(m, q, peer(d))
            fwdcopy(m, q, d).start()
        for c in range(chips):
            agwait(m, q, 2 * c + 1 - core)
        squares = jnp.zeros(sq.shape, jnp.float32) if q == 0 else sq[...]
        lanes = sq.shape[1]
        for o in range(parts):
            x = xall[m, q, o].astype(jnp.float32)
            for lane in range(0, chunk, lanes):
                piece = x[:, lane : lane + lanes]
                squares = squares + piece * piece
            xs[:, o * chunk : (o + 1) * chunk] = (x * gain[o, q]).astype(jnp.bfloat16)
        sq[...] = squares
        gcopy(i).wait()
        ucopy(i).wait()

        def block(fb, carry):
            cols = pl.ds(pl.multiple_of(fb * fb_size, fb_size), fb_size)
            for acc, buf in ((accg, wgb), (accu, wub)):
                w = buf[i % 2, :, :, cols].reshape(parts * chunk, fb_size)
                term = jnp.dot(xs[...], w, preferred_element_type=jnp.float32)
                acc[fb] = term if q == 0 else acc[fb] + term
            return carry

        lax.fori_loop(0, n_fb, block, 0)
        if i + 2 < total_steps:
            gcopy(i + 2).start()
            ucopy(i + 2).start()

    def act_step():
        mean = jnp.sum(sq[...], axis=1, keepdims=True) / width
        inverse = lax.rsqrt(mean + norm_eps)

        def block(fb, carry):
            cols = pl.ds(pl.multiple_of(fb * fb_size, fb_size), fb_size)
            g = accg[fb] * inverse
            u = accu[fb] * inverse
            hid[:, cols] = (g / (1.0 + jnp.exp(-g)) * u).astype(jnp.bfloat16)
            return carry

        lax.fori_loop(0, n_fb, block, 0)

    def down(q, owner):
        return lax.dot_general(
            hid[...], wdb[q, owner], (((1,), (1,)), ((), ())), preferred_element_type=jnp.float32
        )

    def finish(m, q):
        sibcopy(m, q, chip).wait_recv()
        new = pown[q % 2, 0] + sibr[m, q, chip].astype(jnp.float32)
        for d in range(1, chips):
            crcopy(m, q, d).wait_recv()
            new = new + crr[m, q, d - 1].astype(jnp.float32)
        new = xall[m, q, me].astype(jnp.float32) + new
        rounded = new.astype(jnp.bfloat16)
        out[m, q] = rounded
        here = pooled.shape[2]
        grouped = rounded.astype(jnp.float32).reshape(here, tokens // here, chunk)
        pooled[m, q] = jnp.sum(grouped, axis=1) / (tokens // here)

        @pl.when(sec < sections - 1)
        def _():
            zcopy(m, q).start()

    def down_step(m, q):
        if m == 0:
            dcopy(q).wait()

        def to_sibling(c, carry):
            sibs[m, q, c] = down(q, 2 * c + 1 - core).astype(jnp.bfloat16)
            sibcopy(m, q, c).start()
            return carry

        lax.fori_loop(0, chips, to_sibling, 0)

        def to_own(d, carry):
            pown[q % 2, d] = down(q, peer(d))
            return carry

        lax.fori_loop(0, chips, to_own, 0)
        for d in range(1, chips):
            c = lax.rem(chip + d, chips)
            sibcopy(m, q, c).wait_recv()
            both = pown[q % 2, d] + sibr[m, q, c].astype(jnp.float32)
            crs[m, q, d - 1] = both.astype(jnp.bfloat16)
            crcopy(m, q, d).start()
        if q > 0:
            finish(m, q - 1)

    pairs = [(m, q) for m in range(batches) for q in range(steps)]

    @pl.when(sec == sections - 1)
    def _():
        for m, q in pairs:
            if sections > 1:
                ecopy(m, q, x0.at[m, q]).start()

    @pl.when((sec > 0) & (sec < sections - 1))
    def _():
        for m, q in pairs:
            ecopy(m, q, x0.at[m, q]).wait_recv()
            ering[m, q] = ering[m, q] + x0[m, q]
            ecopy(m, q, ering.at[m, q]).start()

    for m in range(batches):
        own_arrive(m, 0)
        for q in range(steps):
            gate_step(m, q)
        act_step()
        for q in range(steps):
            down_step(m, q)
        finish(m, steps - 1)

    for m in range(batches):
        for q in range(steps):
            for c in range(chips):
                agcopy(m, q, c).wait_send()
                sibcopy(m, q, c).wait_send()
            for d in range(1, chips):
                fwdcopy(m, q, d).wait_send()
                crcopy(m, q, d).wait_send()

    @pl.when(sec < sections - 1)
    def _():
        for m, q in pairs:
            zcopy(m, q).wait_send()

    @pl.when(sec > 0)
    def _():
        for m, q in pairs:
            ecopy(m, q, x0.at[m, q]).wait_send()


def pipeline(embedded, gain, w_gate, w_up, w_down, responses):
    sections = lax.axis_size("section")
    parts = lax.axis_size("mp")
    chips = parts // 2
    all_tokens, local = embedded.shape
    hidden = w_gate.shape[1]
    width = gain.shape[0]
    batches = BATCHES
    tokens = all_tokens // batches
    chunk = min(CHUNK, local)
    steps = local // chunk
    fb_size = next(size for size in (512, 256, 128, hidden) if hidden % size == 0)
    x0 = embedded.reshape(batches, tokens, steps, chunk).transpose(0, 2, 1, 3)
    split = (parts, steps, chunk, hidden)
    bf16, f32 = jnp.bfloat16, jnp.float32
    vmem = pl.BlockSpec(memory_space=pltpu.VMEM)
    hbm = pl.BlockSpec(memory_space=pltpu.MemorySpace.HBM)
    dma = pltpu.SemaphoreType.DMA
    per_chip = (batches, steps, chips)
    others = max(1, chips - 1)
    tile = (tokens, chunk)
    pooled = pl.pallas_call(
        functools.partial(pipe_kernel, sections, parts),
        out_shape=jax.ShapeDtypeStruct((batches, steps, responses // batches, chunk), f32),
        in_specs=[vmem, vmem, hbm, hbm, hbm],
        out_specs=vmem,
        scratch_shapes=[
            pltpu.VMEM(x0.shape, bf16),
            pltpu.VMEM((batches, steps, parts) + tile, bf16),
            pltpu.VMEM((2, parts, chunk, hidden), bf16),
            pltpu.VMEM((2, parts, chunk, hidden), bf16),
            pltpu.VMEM((steps, parts, chunk, hidden), bf16),
            pltpu.VMEM((hidden // fb_size, tokens, fb_size), f32),
            pltpu.VMEM((hidden // fb_size, tokens, fb_size), f32),
            pltpu.VMEM((tokens, hidden), bf16),
            pltpu.VMEM((tokens, parts * chunk), bf16),
            pltpu.VMEM((tokens, min(128, chunk)), f32),
            pltpu.VMEM(per_chip + tile, bf16),
            pltpu.VMEM(per_chip + tile, bf16),
            pltpu.VMEM((batches, steps, others) + tile, bf16),
            pltpu.VMEM((batches, steps, others) + tile, bf16),
            pltpu.VMEM((2, chips) + tile, f32),
            dma((2,)),
            dma((2,)),
            dma((steps,)),
            pltpu.VMEM(x0.shape, bf16),
            dma((batches, steps)),
            dma((batches, steps)),
            dma((batches, steps)),
            dma((batches, steps)),
            dma(per_chip),
            dma((batches, steps, parts)),
            dma(per_chip),
            dma(per_chip),
            dma(per_chip),
            dma(per_chip),
            dma(per_chip),
        ],
        compiler_params=pltpu.CompilerParams(
            collective_id=0, has_side_effects=True, vmem_limit_bytes=67043328
        ),
    )(
        x0,
        gain.reshape(parts, steps, 1, chunk),
        w_gate.reshape(split),
        w_up.reshape(split),
        w_down.reshape(split),
    )
    return pooled.transpose(1, 3, 0, 2).reshape(local, responses)


def per_device(
    token_ids,
    members,
    owners,
    embed_table,
    norm_gain,
    gate_weight,
    up_weight,
    down_weight,
    final_gain,
    head_weight,
):
    sections = lax.axis_size("section")
    section = lax.axis_index("section")
    vocab_part = embed_table.shape[1]
    flat = token_ids.reshape(-1)
    local_ids = flat - section * vocab_part
    places = jnp.arange(vocab_part, dtype=jnp.int32)
    chosen_ids = (local_ids[:, None] == places[None, :]).astype(jnp.bfloat16)
    picked = lax.dot_general(
        chosen_ids, embed_table, (((1,), (1,)), ((), ())), preferred_element_type=jnp.float32
    )
    pooled = pipeline(
        picked.astype(jnp.bfloat16),
        norm_gain[0],
        gate_weight[0],
        up_weight[0],
        down_weight[0],
        token_ids.shape[0],
    )
    responses_here = token_ids.shape[0]
    groups_count = lax.axis_size("dp")
    parts = lax.axis_size("mp")
    stacked = lax.all_gather(pooled[None], ("dp", "mp"), axis=0, tiled=True)
    stacked = stacked.reshape(groups_count, parts, pooled.shape[0], responses_here)
    everyone = jnp.transpose(stacked, (1, 2, 0, 3)).reshape(
        parts * pooled.shape[0], groups_count * responses_here
    )
    factor = lax.rsqrt(jnp.mean(everyone * everyone, axis=0, keepdims=True) + final_eps)
    normed = (everyone * factor * final_gain[:, None]).astype(jnp.bfloat16)
    head_cols = head_weight.shape[1]
    projected = contract_rows(head_weight, normed)
    mine = lax.dynamic_slice_in_dim(normed, lax.axis_index("mp") * head_cols, head_cols).astype(
        jnp.float32
    )
    partial_scores = lax.dot_general(
        projected,
        mine,
        (((0,), (0,)), ((), ())),
        precision=lax.Precision.HIGHEST,
        preferred_element_type=jnp.float32,
    )
    scores = lax.psum(
        jnp.where(section == sections - 1, partial_scores, jnp.zeros_like(partial_scores)),
        ("section", "mp"),
    )
    preference = jax.nn.sigmoid(scores - scores.T)
    prompt_count = owners.shape[0]
    local_prompts = prompt_count // lax.axis_size("dp")
    rows_local = GROUP // sections
    slot_here = lax.axis_index("dp") * local_prompts + jnp.arange(local_prompts, dtype=jnp.int32)
    match = (owners[None, :] == slot_here[:, None]).astype(jnp.int32)
    prompt_here = jnp.sum(match * jnp.arange(prompt_count, dtype=jnp.int32)[None, :], axis=1)
    groups = members.reshape(prompt_count, GROUP)
    chosen = groups[prompt_here]
    row_ids = lax.dynamic_slice_in_dim(chosen, section * rows_local, rows_local, 1)
    return preference[row_ids[:, :, None], chosen[:, None, :]]


def solution(mesh):
    placed = (
        P("dp", None),
        P(),
        P(),
        P("mp", "section"),
        P("section", None),
        P("section", None, "mp"),
        P("section", None, "mp"),
        P("section", None, "mp"),
        P(),
        P(None, "mp"),
    )
    return jax.shard_map(
        per_device, mesh=mesh, in_specs=placed, out_specs=P("dp", "section", None), check_vma=False
    )
```

```python
import functools

import jax
import jax.numpy as jnp
from jax import lax
from jax.experimental import pallas as pl
from jax.experimental.pallas import tpu as pltpu
from jax.sharding import PartitionSpec as P

GROUP = 8
BATCHES = 2
CHUNK = 256

norm_eps = 1e-05
final_eps = 1e-06
MESH = pl.DeviceIdType.MESH


def contract_rows(weights, acts):
    return lax.dot_general(
        weights, acts, (((0,), (0,)), ((), ())), preferred_element_type=jnp.float32
    )


def pipe_kernel(
    sections,
    parts,
    x0,
    gain,
    wg,
    wu,
    wd,
    pooled,
    out,
    xall,
    wgb,
    wub,
    wdb,
    accg,
    accu,
    hid,
    xs,
    sq,
    sibs,
    sibr,
    crs,
    crr,
    pown,
    gsem,
    usem,
    dsem,
    ering,
    esend,
    erecv,
    zsend,
    zrecv,
    agsend,
    agrecv,
    fwdsend,
    sibsend,
    sibrecv,
    crsend,
    crrecv,
):
    batches, steps, tokens, chunk = x0.shape
    chips = parts // 2
    width = parts * steps * chunk
    n_fb, _, fb_size = accg.shape
    sec = lax.axis_index("section")
    me = lax.axis_index("mp")
    core = lax.rem(me, 2)
    chip = lax.div(me, 2)
    sib = me + 1 - 2 * core

    def peer(d):
        return lax.rem(chip + d, chips) * 2 + core

    def remote(src, dst, send, recv, target):
        return pltpu.make_async_remote_copy(
            src_ref=src,
            dst_ref=dst,
            send_sem=send,
            recv_sem=recv,
            device_id=target,
            device_id_type=MESH,
        )

    def order(m):
        return list(range(steps)) if m % 2 == 0 else list(range(steps))[::-1]

    visits = [q for m in range(batches) for q in order(m)]
    held = [None, None]
    slots, fresh = [], []
    for i, q in enumerate(visits):
        fresh.append(q not in held)
        if q not in held:
            free = [n for n in range(2) if held[n] not in visits[i - 1 : i] or held[n] is None]
            held[free[0]] = q
        slots.append(held.index(q))

    def gcopy(i):
        slot = slots[i]
        return pltpu.make_async_copy(wg.at[:, visits[i]], wgb.at[slot], gsem.at[slot])

    def ucopy(i):
        slot = slots[i]
        return pltpu.make_async_copy(wu.at[:, visits[i]], wub.at[slot], usem.at[slot])

    def load_into(slot, after):
        for i in range(after, len(visits)):
            if slots[i] == slot:
                if fresh[i]:
                    gcopy(i).start()
                    ucopy(i).start()
                return

    def dcopy(q):
        return pltpu.make_async_copy(wd.at[:, q], wdb.at[q], dsem.at[q])

    def ecopy(m, q, src):
        target = {"section": sec - 1}
        return remote(src, ering.at[m, q], esend.at[m, q], erecv.at[m, q], target)

    def zcopy(m, q):
        return remote(
            out.at[m, q], xall.at[m, q, me], zsend.at[m, q], zrecv.at[m, q], {"section": sec + 1}
        )

    def agcopy(m, q, d):
        slot = xall.at[m, q, me]
        target = sib if d == 0 else peer(d)
        return remote(slot, slot, agsend.at[m, q, d], agrecv.at[m, q, me], {"mp": target})

    def fwdcopy(m, q, d):
        slot = xall.at[m, q, peer(d)]
        return remote(slot, slot, fwdsend.at[m, q, d], agrecv.at[m, q, peer(d)], {"mp": sib})

    def agwait(m, q, owner):
        slot = xall.at[m, q, owner]
        remote(slot, slot, agsend.at[m, q, 0], agrecv.at[m, q, owner], {"mp": sib}).wait_recv()

    def sibcopy(m, q, c):
        return remote(
            sibs.at[m, q, c], sibr.at[m, q, c], sibsend.at[m, q, c], sibrecv.at[m, q, c], {"mp": sib}
        )

    def crcopy(m, q, d):
        return remote(
            crs.at[m, q, d - 1],
            crr.at[m, q, d - 1],
            crsend.at[m, q, d - 1],
            crrecv.at[m, q, d - 1],
            {"mp": peer(d)},
        )

    for slot in range(2):
        load_into(slot, 0)

    barrier = pltpu.get_barrier_semaphore()
    pl.semaphore_signal(barrier, inc=1, device_id={"mp": sib}, device_id_type=MESH)
    for d in range(1, chips):
        pl.semaphore_signal(barrier, inc=1, device_id={"mp": peer(d)}, device_id_type=MESH)

    for turn in (1, sections - 1):
        around = lax.rem(sec + turn, sections)
        pl.semaphore_signal(barrier, inc=1, device_id={"section": around}, device_id_type=MESH)
    pl.semaphore_wait(barrier, chips + 2)

    def own_arrive(m, q):
        @pl.when(sec == 0)
        def _():
            if sections > 1:
                ecopy(m, q, x0.at[m, q]).wait_recv()
                xall[m, q, me] = ering[m, q] + x0[m, q]
            else:
                xall[m, q, me] = x0[m, q]

        @pl.when(sec > 0)
        def _():
            zcopy(m, q).wait_recv()

        for d in range(1, chips):
            agcopy(m, q, d).start()
        agcopy(m, q, 0).start()

    def gate_step(m, turn):
        i = m * steps + turn
        q, slot = visits[i], slots[i]
        if turn + 1 < steps:
            own_arrive(m, visits[i + 1])
        for d in range(1, chips):
            agwait(m, q, peer(d))
            fwdcopy(m, q, d).start()
        for c in range(chips):
            agwait(m, q, 2 * c + 1 - core)
        squares = jnp.zeros(sq.shape, jnp.float32) if turn == 0 else sq[...]
        lanes = sq.shape[1]
        for o in range(parts):
            x = xall[m, q, o].astype(jnp.float32)
            for lane in range(0, chunk, lanes):
                piece = x[:, lane : lane + lanes]
                squares = squares + piece * piece
            xs[:, o * chunk : (o + 1) * chunk] = (x * gain[o, q]).astype(jnp.bfloat16)
        sq[...] = squares
        if fresh[i]:
            gcopy(i).wait()
            ucopy(i).wait()

        def block(fb, carry):
            cols = pl.ds(pl.multiple_of(fb * fb_size, fb_size), fb_size)
            for acc, buf in ((accg, wgb), (accu, wub)):
                w = buf[slot, :, :, cols].reshape(parts * chunk, fb_size)
                term = jnp.dot(xs[...], w, preferred_element_type=jnp.float32)
                acc[fb] = term if turn == 0 else acc[fb] + term
            return carry

        lax.fori_loop(0, n_fb, block, 0)
        load_into(slot, i + 1)
        if m == 0 and turn == min(1, steps - 1):
            for other in range(steps):
                dcopy(other).start()

    def act_step():
        mean = jnp.sum(sq[...], axis=1, keepdims=True) / width
        inverse = lax.rsqrt(mean + norm_eps)

        def block(fb, carry):
            cols = pl.ds(pl.multiple_of(fb * fb_size, fb_size), fb_size)
            g = accg[fb] * inverse
            u = accu[fb] * inverse
            hid[:, cols] = (g / (1.0 + jnp.exp(-g)) * u).astype(jnp.bfloat16)
            return carry

        lax.fori_loop(0, n_fb, block, 0)

    def down(q, owner):
        return lax.dot_general(
            hid[...], wdb[q, owner], (((1,), (1,)), ((), ())), preferred_element_type=jnp.float32
        )

    def finish(m, q):
        sibcopy(m, q, chip).wait_recv()
        new = pown[q % 2, 0] + sibr[m, q, chip].astype(jnp.float32)
        for d in range(1, chips):
            crcopy(m, q, d).wait_recv()
            new = new + crr[m, q, d - 1].astype(jnp.float32)
        new = xall[m, q, me].astype(jnp.float32) + new
        rounded = new.astype(jnp.bfloat16)
        out[m, q] = rounded
        here = pooled.shape[2]
        grouped = rounded.astype(jnp.float32).reshape(here, tokens // here, chunk)
        pooled[m, q] = jnp.sum(grouped, axis=1) / (tokens // here)

        @pl.when(sec < sections - 1)
        def _():
            zcopy(m, q).start()

    def down_step(m, turn):
        q = order(m)[turn]
        if m == 0:
            dcopy(q).wait()

        def to_sibling(c, carry):
            sibs[m, q, c] = down(q, 2 * c + 1 - core).astype(jnp.bfloat16)
            sibcopy(m, q, c).start()
            return carry

        lax.fori_loop(0, chips, to_sibling, 0)

        def to_own(d, carry):
            pown[q % 2, d] = down(q, peer(d))
            return carry

        lax.fori_loop(0, chips, to_own, 0)
        for d in range(1, chips):
            c = lax.rem(chip + d, chips)
            sibcopy(m, q, c).wait_recv()
            both = pown[q % 2, d] + sibr[m, q, c].astype(jnp.float32)
            crs[m, q, d - 1] = both.astype(jnp.bfloat16)
            crcopy(m, q, d).start()
        if turn > 0:
            finish(m, order(m)[turn - 1])

    pairs = [(m, q) for m in range(batches) for q in order(m)]

    @pl.when(sec == sections - 1)
    def _():
        for m, q in pairs:
            if sections > 1:
                ecopy(m, q, x0.at[m, q]).start()

    @pl.when((sec > 0) & (sec < sections - 1))
    def _():
        for m, q in pairs:
            ecopy(m, q, x0.at[m, q]).wait_recv()
            ering[m, q] = ering[m, q] + x0[m, q]
            ecopy(m, q, ering.at[m, q]).start()

    for m in range(batches):
        own_arrive(m, order(m)[0])
        for turn in range(steps):
            gate_step(m, turn)
        act_step()
        for turn in range(steps):
            down_step(m, turn)
        finish(m, order(m)[-1])

    for m in range(batches):
        for q in range(steps):
            for c in range(chips):
                agcopy(m, q, c).wait_send()
                sibcopy(m, q, c).wait_send()
            for d in range(1, chips):
                fwdcopy(m, q, d).wait_send()
                crcopy(m, q, d).wait_send()

    @pl.when(sec < sections - 1)
    def _():
        for m, q in pairs:
            zcopy(m, q).wait_send()

    @pl.when(sec > 0)
    def _():
        for m, q in pairs:
            ecopy(m, q, x0.at[m, q]).wait_send()


def pipeline(embedded, gain, w_gate, w_up, w_down, responses):
    sections = lax.axis_size("section")
    parts = lax.axis_size("mp")
    chips = parts // 2
    all_tokens, local = embedded.shape
    hidden = w_gate.shape[1]
    width = gain.shape[0]
    batches = BATCHES
    tokens = all_tokens // batches
    chunk = min(CHUNK, local)
    steps = local // chunk
    fb_size = next(size for size in (512, 256, 128, hidden) if hidden % size == 0)
    x0 = embedded.reshape(batches, tokens, steps, chunk).transpose(0, 2, 1, 3)
    split = (parts, steps, chunk, hidden)
    bf16, f32 = jnp.bfloat16, jnp.float32
    vmem = pl.BlockSpec(memory_space=pltpu.VMEM)
    hbm = pl.BlockSpec(memory_space=pltpu.MemorySpace.HBM)
    dma = pltpu.SemaphoreType.DMA
    per_chip = (batches, steps, chips)
    others = max(1, chips - 1)
    tile = (tokens, chunk)
    pooled = pl.pallas_call(
        functools.partial(pipe_kernel, sections, parts),
        out_shape=jax.ShapeDtypeStruct((batches, steps, responses // batches, chunk), f32),
        in_specs=[vmem, vmem, hbm, hbm, hbm],
        out_specs=vmem,
        scratch_shapes=[
            pltpu.VMEM(x0.shape, bf16),
            pltpu.VMEM((batches, steps, parts) + tile, bf16),
            pltpu.VMEM((2, parts, chunk, hidden), bf16),
            pltpu.VMEM((2, parts, chunk, hidden), bf16),
            pltpu.VMEM((steps, parts, chunk, hidden), bf16),
            pltpu.VMEM((hidden // fb_size, tokens, fb_size), f32),
            pltpu.VMEM((hidden // fb_size, tokens, fb_size), f32),
            pltpu.VMEM((tokens, hidden), bf16),
            pltpu.VMEM((tokens, parts * chunk), bf16),
            pltpu.VMEM((tokens, min(128, chunk)), f32),
            pltpu.VMEM(per_chip + tile, bf16),
            pltpu.VMEM(per_chip + tile, bf16),
            pltpu.VMEM((batches, steps, others) + tile, bf16),
            pltpu.VMEM((batches, steps, others) + tile, bf16),
            pltpu.VMEM((2, chips) + tile, f32),
            dma((2,)),
            dma((2,)),
            dma((steps,)),
            pltpu.VMEM(x0.shape, bf16),
            dma((batches, steps)),
            dma((batches, steps)),
            dma((batches, steps)),
            dma((batches, steps)),
            dma(per_chip),
            dma((batches, steps, parts)),
            dma(per_chip),
            dma(per_chip),
            dma(per_chip),
            dma(per_chip),
            dma(per_chip),
        ],
        compiler_params=pltpu.CompilerParams(
            collective_id=0, has_side_effects=True, vmem_limit_bytes=67043328
        ),
    )(
        x0,
        gain.reshape(parts, steps, 1, chunk),
        w_gate.reshape(split),
        w_up.reshape(split),
        w_down.reshape(split),
    )
    return pooled.transpose(1, 3, 0, 2).reshape(local, responses)


def per_device(
    token_ids,
    members,
    owners,
    embed_table,
    norm_gain,
    gate_weight,
    up_weight,
    down_weight,
    final_gain,
    head_weight,
):
    sections = lax.axis_size("section")
    section = lax.axis_index("section")
    vocab_part = embed_table.shape[1]
    flat = token_ids.reshape(-1)
    local_ids = flat - section * vocab_part
    places = jnp.arange(vocab_part, dtype=jnp.int32)
    chosen_ids = (local_ids[:, None] == places[None, :]).astype(jnp.bfloat16)
    picked = lax.dot_general(
        chosen_ids, embed_table, (((1,), (1,)), ((), ())), preferred_element_type=jnp.float32
    )
    pooled = pipeline(
        picked.astype(jnp.bfloat16),
        norm_gain[0],
        gate_weight[0],
        up_weight[0],
        down_weight[0],
        token_ids.shape[0],
    )
    responses_here = token_ids.shape[0]
    groups_count = lax.axis_size("dp")
    parts = lax.axis_size("mp")
    stacked = lax.all_gather(pooled[None], ("dp", "mp"), axis=0, tiled=True)
    stacked = stacked.reshape(groups_count, parts, pooled.shape[0], responses_here)
    everyone = jnp.transpose(stacked, (1, 2, 0, 3)).reshape(
        parts * pooled.shape[0], groups_count * responses_here
    )
    factor = lax.rsqrt(jnp.mean(everyone * everyone, axis=0, keepdims=True) + final_eps)
    normed = (everyone * factor * final_gain[:, None]).astype(jnp.bfloat16)
    head_cols = head_weight.shape[1]
    projected = contract_rows(head_weight, normed)
    mine = lax.dynamic_slice_in_dim(normed, lax.axis_index("mp") * head_cols, head_cols).astype(
        jnp.float32
    )
    partial_scores = lax.dot_general(
        projected,
        mine,
        (((0,), (0,)), ((), ())),
        precision=lax.Precision.HIGHEST,
        preferred_element_type=jnp.float32,
    )
    shares = lax.all_gather(partial_scores[None], ("section", "mp"), axis=0, tiled=True)
    scores = jnp.sum(shares[(sections - 1) * parts :], axis=0)
    preference = jax.nn.sigmoid(scores - scores.T)
    prompt_count = owners.shape[0]
    local_prompts = prompt_count // lax.axis_size("dp")
    rows_local = GROUP // sections
    slot_here = lax.axis_index("dp") * local_prompts + jnp.arange(local_prompts, dtype=jnp.int32)
    match = (owners[None, :] == slot_here[:, None]).astype(jnp.int32)
    prompt_here = jnp.sum(match * jnp.arange(prompt_count, dtype=jnp.int32)[None, :], axis=1)
    groups = members.reshape(prompt_count, GROUP)
    chosen = groups[prompt_here]
    row_ids = lax.dynamic_slice_in_dim(chosen, section * rows_local, rows_local, 1)
    return preference[row_ids[:, :, None], chosen[:, None, :]]


def solution(mesh):
    placed = (
        P("dp", None),
        P(),
        P(),
        P("mp", "section"),
        P("section", None),
        P("section", None, "mp"),
        P("section", None, "mp"),
        P("section", None, "mp"),
        P(),
        P(None, "mp"),
    )
    return jax.shard_map(
        per_device, mesh=mesh, in_specs=placed, out_specs=P("dp", "section", None), check_vma=False
    )
```
